512 devices in a mesh: fsdp: 16 (over x, z_lo), space: 32 (over y, z_hi, core).
Axes of the slice: x: 4, y: 8, z: 8 (z_hi: 2, z_lo: 4; z = z_hi * 4 + z_lo), core: 2. Of those that a mesh axis runs over, the one named last changes fastest.
Arguments:
- images: bfloat16 [16, 768, 128, 256], P('fsdp', 'space'), may hold values from -6 to 6
- kernel: bfloat16 [256, 3, 3, 256], P('fsdp'), may hold values from -0.125 to 0.125
- cotangent: bfloat16 [16, 384, 64, 256], P('fsdp', 'space'), may hold values from -6 to 6
Outputs:
- output: bfloat16 [16, 384, 64, 256], P('fsdp', 'space')
- grad_input: bfloat16 [16, 768, 128, 256], P('fsdp', 'space')
- grad_kernel: float32 [256, 3, 3, 256], P('fsdp', None, None, 'space')
- penalty_rows: float32 [256], P('fsdp')
The draws below stay inside these ranges and needn't reach their ends.
All inputs are finite; a program needn't handle non-finite values.
Results may differ from the reference program's by a relative error of at most 0.0034.
Values may be sent and summed in bfloat16 or wider, within the bound.
No kernel may reach another device: no remote copies, remote signals or barrier semaphores. Data moves between devices by JAX's collectives and lax.ppermute only.
A program may use at most 64 MiB of HBM per device.

```python
import jax
import jax.numpy as jnp
from jax import lax

C_IN = 256
C_OUT = 256
COLS = 128
STRIPS = 16
H = 768
OUT_ROWS = 384
OUT_COLS = 64


def strengthened(array, stream_key, source, target, blocks, factor):
    def block_of(position):
        return (jnp.arange(array.shape[position]) // (array.shape[position] // blocks)).reshape((-1,) + (1,) * (array.ndim - 1 - position))

    near = jax.random.permutation(stream_key, blocks)[block_of(target)]
    second = (block_of(target) + blocks // 2) % blocks
    return jnp.where((block_of(source) == near) | (block_of(source) == second), factor * array, array)


def block_scale(rng, shape, split, smallest, top_value):
    loudness, own = 1.0, jax.random.fold_in(rng, 6)
    for position, blocks in split:
        draws = jnp.exp(jax.random.uniform(jax.random.fold_in(own, position), (blocks,), jnp.float32, smallest / len(split), top_value / len(split)))
        loudness = loudness * jnp.repeat(draws, shape[position] // blocks).reshape([-1 if axis == position else 1 for axis in range(len(shape))])
    return loudness


def bell_draw(key, shape, scale, bound, pieces=(), kind=jnp.bfloat16):
    values = jax.random.normal(key, shape, jnp.float32) * scale
    if len(pieces) > 0:
        values = block_scale(key, shape, pieces, -0.22, 0.18) * values
    return jnp.clip(values, min=-bound, max=bound).astype(kind)


def gaussian_with(own_key, dims, scale, most, pieces, heavy, dtype=jnp.bfloat16):
    array = scale * jax.random.normal(own_key, dims, jnp.float32)
    if pieces:
        array = array * block_scale(own_key, dims, pieces, -0.22, 0.18)
    return jnp.clip(strengthened(array, jax.random.fold_in(own_key, 3), *heavy), -most, most).astype(dtype)


def setup_inputs(seed: int = 0) -> dict:
    key_of = jax.random.split(jax.random.key(seed), 4)
    return {
        "images": gaussian_with(key_of[0], (STRIPS, H, COLS, C_IN), 1.0, 6.0, ((0, 16), (1, 32)), (1, 3, 32, 2.75)),
        "kernel": bell_draw(key_of[1], (C_OUT, 3, 3, C_IN), (9 * C_IN) ** -0.5, 0.125, ((0, 16),)),
        "cotangent": gaussian_with(key_of[2], (STRIPS, OUT_ROWS, OUT_COLS, C_OUT), 1.0, 6.0, ((0, 16), (1, 32)), (0, 3, 16, 2.0)),
    }


PEN_WEIGHT = 4.0

def conv_strip(strip_in, weights):
    return lax.conv_general_dilated(strip_in[None], weights, (2, 2), ((1, 0), (1, 0)), dimension_numbers=('NHWC', 'OHWI', 'NHWC'), precision=lax.Precision.HIGHEST)[0]

def shifted(padded, row_shift, col_shift):
    return padded[:, 2 + row_shift:5 + row_shift, 2 + col_shift:5 + col_shift, :]

def penalty_terms(own_panel, gathered, first_row):
    own_count = own_panel.shape[0]
    channels = gathered.shape[0]
    spread = ((0, 0), (2, 2), (2, 2), (0, 0))
    own_pad = jnp.pad(own_panel, spread)
    whole_pad = jnp.pad(gathered, spread)
    whole_flat = gathered.reshape(channels, -1)
    identity_rows = (lax.broadcasted_iota(jnp.int32, (own_count, channels), 0) + first_row == lax.broadcasted_iota(jnp.int32, (own_count, channels), 1)).astype(jnp.float32)
    row_penalty = jnp.zeros((own_count,), jnp.float32)
    pen_grad = jnp.zeros((own_count, whole_flat.shape[1]), jnp.float32)
    for row_shift in (-2, 0, 2):
        for col_shift in (-2, 0, 2):
            moved_rows = shifted(own_pad, row_shift, col_shift).reshape(own_count, -1)
            gram_block = lax.dot_general(moved_rows, whole_flat, (((1,), (1,)), ((), ())), preferred_element_type=jnp.float32)
            if row_shift == 0 and col_shift == 0:
                gram_block = gram_block - identity_rows
            row_penalty = row_penalty + lax.optimization_barrier(jnp.sum(gram_block * gram_block, axis=1))
            back_flat = shifted(whole_pad, -row_shift, -col_shift).reshape(channels, -1).astype(jnp.float32)
            pen_grad = pen_grad + jnp.dot(gram_block, back_flat, precision=lax.Precision.HIGHEST)
    return (row_penalty, 4.0 * pen_grad.reshape(own_panel.shape))

def reference(images, kernel, cotangent):
    weights = kernel.astype(jnp.float32)

    def per_strip(grad_total, strip_pair):
        strip_in, grad_out = strip_pair
        result, pull_back = jax.vjp(conv_strip, strip_in.astype(jnp.float32), weights)
        grad_strip, grad_weights = pull_back(grad_out.astype(jnp.float32))
        return (grad_total + grad_weights, (result.astype(jnp.bfloat16), grad_strip.astype(jnp.bfloat16)))
    grad_total, (output, grad_input) = lax.scan(per_strip, jnp.zeros(kernel.shape, jnp.float32), (images, cotangent))
    penalty_rows, penalty_grad = penalty_terms(kernel, kernel, 0)
    grad_kernel = grad_total / OUT_ROWS + PEN_WEIGHT * penalty_grad
    return (output, grad_input, grad_kernel, penalty_rows)
```

```python
import jax
import jax.numpy as jnp
from jax import lax
from jax.experimental import pallas as pl
from jax.experimental.pallas import tpu as pltpu
from jax.sharding import Mesh, PartitionSpec as P

PEN_WEIGHT = 4.0
BF = jnp.bfloat16
F32 = jnp.float32

ROWS, COLS, CH = 24, 128, 256
R, Q = 12, 64
POS = R * Q
TAPS = [(i, j) for i in range(3) for j in range(3)]
SHIFTS = [(u, v) for u in (-2, 0, 2) for v in (-2, 0, 2)]

NT = (((1,), (1,)), ((), ()))


def mm(a, b):
    return jnp.dot(a, b, preferred_element_type=F32)


def mm_nt(a, b):
    return lax.dot_general(a, b, NT, preferred_element_type=F32)


def one_hot(cond):
    return jnp.where(cond, 1.0, 0.0).astype(BF)


def iota2(shape, axis):
    return lax.broadcasted_iota(jnp.int32, shape, axis)


def column_sorter():
    row, col = iota2((COLS, COLS), 0), iota2((COLS, COLS), 1)
    return one_hot(col == 2 * (row % Q) + row // Q)


def shift_left(block):
    moved = pltpu.roll(block, Q - 1, 0)
    return jnp.where(iota2(block.shape, 0) == Q - 1, 0.0, moved)


def shift_right(block):
    moved = pltpu.roll(block, 1, 0)
    return jnp.where(iota2(block.shape, 0) == 0, 0.0, moved)


def wgrad_kernel(
    core_ref, img_ref, cot_ref, low_ref,
    keep_ref, send_ref, ee_ref, eo_ref, oe_ref, oo_ref, cot_s_ref,
    per_ref, cot_t_ref,
):
    core = core_ref[0]
    sorter = column_sorter()
    chan, slot = iota2((CH, CH), 0), iota2((CH, CH), 1)
    other = jnp.where((chan // 8) % 2 == core, 0, 1)
    to_core = one_hot(slot == (chan // 16) * 8 + chan % 8 + (CH // 2) * other)
    for r in range(R):
        for parity, (even_ref, odd_ref) in enumerate(((ee_ref, eo_ref), (oe_ref, oo_ref))):
            split = mm(sorter, img_ref[2 * r + parity]).astype(BF)
            even_ref[r * Q : (r + 1) * Q] = split[:Q]
            odd_ref[r * Q : (r + 1) * Q] = split[Q:]
    for k, ref in enumerate((ee_ref, eo_ref, oe_ref, oo_ref)):
        per_ref[k] = mm(ref[...], to_core).astype(BF)
    for r in range(R + 1):
        row = cot_ref[r] if r < R else low_ref[...]
        cot_s_ref[r * Q : (r + 1) * Q] = shift_left(row.astype(F32)).astype(BF)
    cot = cot_ref[...].reshape(POS, CH)
    below = jnp.concatenate([cot[Q:], low_ref[...]], axis=0)
    cot_t_ref[0] = cot.T
    cot_t_ref[1] = below.T
    cot_t_ref[2] = cot_s_ref[0:POS].T
    cot_t_ref[3] = cot_s_ref[Q : Q + POS].T
    for t, (i, j) in enumerate(TAPS):
        grad_rows = (1 if i == 0 else 0) + (2 if j == 0 else 0)
        image = (0 if i == 1 else 2) + (0 if j == 1 else 1)
        tap = mm(cot_t_ref[grad_rows], per_ref[image]).reshape(16, 16, CH)
        keep_ref[:, t] = tap[:, :, : CH // 2]
        send_ref[:, t] = tap[:, :, CH // 2 :].astype(BF)


def conv_kernel(
    place_ref, mine_ref, other_ref, up_ref, low_ref, cot_ref, cot_s_ref,
    ee_ref, eo_ref, oe_ref, oo_ref,
    out_ref, gin_ref, pen_ref, row_ref,
    w_ref, acc_ref, z_ref,
):
    core, x, zl, space = place_ref[0], place_ref[1], place_ref[2], place_ref[3]
    half = CH // 2
    for a, dx in enumerate((0, 1, 3, 2)):
        for b, dz in enumerate((0, 1, 3, 2)):
            first = pl.multiple_of((((x + dx) % 4) * 4 + (zl + dz) % 4) * 16, 16)
            rows = slice((a * 4 + b) * 16, (a * 4 + b + 1) * 16)

            @pl.when(core == 0)
            def _(first=first, rows=rows):
                for t in range(9):
                    lanes = slice(t * half, (t + 1) * half)
                    w_ref[pl.ds(first, 16), t * CH : t * CH + half] = mine_ref[rows, lanes]
                    w_ref[pl.ds(first, 16), t * CH + half : (t + 1) * CH] = other_ref[rows, lanes]

            @pl.when(core == 1)
            def _(first=first, rows=rows):
                for t in range(9):
                    lanes = slice(t * half, (t + 1) * half)
                    w_ref[pl.ds(first, 16), t * CH : t * CH + half] = other_ref[rows, lanes]
                    w_ref[pl.ds(first, 16), t * CH + half : (t + 1) * CH] = mine_ref[rows, lanes]

    def tap(i, j):
        t = 3 * i + j
        return w_ref[:, t * CH : (t + 1) * CH]

    sorter = column_sorter()
    halo = mm(sorter, up_ref[...]).astype(BF)
    oe_up = jnp.concatenate([halo[:Q], oe_ref[0 : POS - Q]], axis=0)
    oo_up = jnp.concatenate([halo[Q:], oo_ref[0 : POS - Q]], axis=0)
    z_ref[...] = mm_nt(eo_ref[...], tap(1, 0))
    z_ref[...] += mm_nt(oo_ref[...], tap(2, 0))
    z_ref[...] += mm_nt(oo_up, tap(0, 0))
    acc_ref[0] = mm_nt(ee_ref[...], tap(1, 1))
    acc_ref[0] += mm_nt(eo_ref[...], tap(1, 2))
    acc_ref[0] += mm_nt(oe_ref[...], tap(2, 1))
    acc_ref[0] += mm_nt(oo_ref[...], tap(2, 2))
    acc_ref[0] += mm_nt(oe_up, tap(0, 1))
    acc_ref[0] += mm_nt(oo_up, tap(0, 2))
    for r in range(R):
        rows = slice(r * Q, (r + 1) * Q)
        out_ref[r] = (acc_ref[0, rows] + shift_right(z_ref[rows])).astype(BF)
    cot = cot_ref[...].reshape(POS, CH)
    below = jnp.concatenate([cot[Q:], low_ref[...]], axis=0)
    cot_s = cot_s_ref[0:POS]
    below_s = cot_s_ref[Q : Q + POS]
    acc_ref[0] = mm(cot, tap(1, 1))
    acc_ref[1] = mm(cot, tap(1, 2))
    acc_ref[1] += mm(cot_s, tap(1, 0))
    acc_ref[2] = mm(cot, tap(2, 1))
    acc_ref[2] += mm(below, tap(0, 1))
    acc_ref[3] = mm(cot, tap(2, 2))
    acc_ref[3] += mm(cot_s, tap(2, 0))
    acc_ref[3] += mm(below, tap(0, 2))
    acc_ref[3] += mm(below_s, tap(0, 0))
    row, col = iota2((COLS, COLS), 0), iota2((COLS, COLS), 1)
    weaver = one_hot(col == (row % 2) * Q + row // 2)
    for r in range(R):
        rows = slice(r * Q, (r + 1) * Q)
        for parity in range(2):
            both = jnp.concatenate(
                [acc_ref[2 * parity, rows].astype(BF), acc_ref[2 * parity + 1, rows].astype(BF)], axis=0
            )
            gin_ref[2 * r + parity] = mm(weaver, both).astype(BF)
    own_first = pl.multiple_of((x * 4 + zl) * 16, 16)
    own = [w_ref[pl.ds(own_first, 16), t * CH : (t + 1) * CH] for t in range(9)]
    grams = {}
    kin = [[s for s in range(9) if (s // 3 - t // 3) % 2 == 0 and (s % 3 - t % 3) % 2 == 0] for t in range(9)]
    for t in range(9):
        stacked = jnp.concatenate([own[s] for s in kin[t]], axis=0)
        part = mm_nt(stacked, w_ref[:, t * CH : (t + 1) * CH])
        for n, s in enumerate(kin[t]):
            shift = (s // 3 - t // 3, s % 3 - t % 3)
            block = part[n * 16 : (n + 1) * 16]
            grams[shift] = grams[shift] + block if shift in grams else block
    diagonal = iota2((16, CH), 0) + own_first == iota2((16, CH), 1)
    grams[(0, 0)] = grams[(0, 0)] - jnp.where(diagonal, 1.0, 0.0)
    squares = jnp.zeros((16, CH), F32)
    for shift in SHIFTS:
        squares = squares + grams[shift] * grams[shift]
    row_ref[...] = jnp.sum(squares, axis=1, keepdims=True)
    pieces = {}
    for shift in SHIFTS:
        high = grams[shift].astype(BF)
        rest = grams[shift] - high.astype(F32)
        mid = rest.astype(BF)
        pieces[shift] = (high, mid, (rest - mid.astype(F32)).astype(BF))
    grads = [jnp.zeros((16, CH), F32) for _ in range(9)]
    for s in range(9):
        stacked = jnp.concatenate(
            [pieces[(t // 3 - s // 3, t % 3 - s % 3)][p] for t in kin[s] for p in range(3)], axis=0
        )
        part = mm(stacked, w_ref[:, s * CH : (s + 1) * CH])
        for n, t in enumerate(kin[s]):
            for p in range(3):
                grads[t] = grads[t] + part[(3 * n + p) * 16 : (3 * n + p + 1) * 16]
    stacked = jnp.concatenate(grads, axis=0)
    high = stacked.astype(BF)
    rest = stacked - high.astype(F32)
    mid = rest.astype(BF)
    low = (rest - mid.astype(F32)).astype(BF)
    pick = one_hot(iota2((8, CH), 0) + space * 8 == iota2((8, CH), 1))
    pen_ref[...] = mm_nt(pick, high) + mm_nt(pick, mid) + mm_nt(pick, low)


def sum_kernel(parts_ref, out_ref):
    total = parts_ref[0].astype(F32)
    for k in range(1, 4):
        total = total + parts_ref[k].astype(F32)
    turned = total.T
    for k in range(4):
        out_ref[:, k] = turned[:, 144 * k : 144 * (k + 1)].reshape(16, 8, 144).astype(BF)


def call(kernel, name, out_shape, scratch=(), n_scalar=0, n_in=0):
    vmem = pl.BlockSpec(memory_space=pltpu.VMEM)
    smem = pl.BlockSpec(memory_space=pltpu.SMEM)
    many = isinstance(out_shape, (tuple, list))
    return pl.pallas_call(
        kernel,
        out_shape=out_shape,
        in_specs=[smem] * n_scalar + [vmem] * n_in,
        out_specs=tuple(vmem for _ in out_shape) if many else vmem,
        scratch_shapes=list(scratch),
        name=name,
        compiler_params=pltpu.CompilerParams(vmem_limit_bytes=48 * 1024 * 1024),
    )


def ring(block, axis, size, distance):
    return lax.ppermute(block, axis, [((i + distance) % size, i) for i in range(size)])


def per_device(images, kernel, cotangent):
    S = jax.ShapeDtypeStruct
    x, zl = lax.axis_index("x"), lax.axis_index("zl")
    core = lax.axis_index("core")
    space = lax.axis_index(("y", "zh", "core"))
    n_space = 32
    images, cotangent = images[0], cotangent[0]
    low = lax.ppermute(cotangent[0], ("y", "zh", "core"), [(i + 1, i) for i in range(n_space - 1)])
    up = lax.ppermute(images[ROWS - 1], ("y", "zh", "core"), [(i, i + 1) for i in range(n_space - 1)])
    panel = lax.dynamic_index_in_dim(kernel.reshape(16, 9, 2, CH // 2), core, 2, keepdims=False)
    panel = panel.reshape(16, 9 * CH // 2)
    zs = jnp.concatenate([panel] + [ring(panel, "zl", 4, d) for d in (1, 3, 2)], axis=0)
    mine = jnp.concatenate([zs] + [ring(zs, "x", 4, d) for d in (1, 3, 2)], axis=0)
    swap = [(0, 1), (1, 0)]
    other = lax.ppermute(mine, "core", swap)

    keep, send, ee, eo, oe, oo, cot_s = call(
        wgrad_kernel,
        "wgrad",
        (S((16, 9, 16, 128), F32), S((16, 9, 16, 128), BF), S((POS, CH), BF), S((POS, CH), BF),
         S((POS, CH), BF), S((POS, CH), BF), S((POS + Q, CH), BF)),
        scratch=[pltpu.VMEM((4, POS, CH), BF), pltpu.VMEM((4, CH, POS), BF)],
        n_scalar=1,
        n_in=3,
    )(core.astype(jnp.int32).reshape(1), images, cotangent, low)
    recv = lax.ppermute(send, "core", swap)
    both = (keep + recv.astype(F32)).astype(BF).reshape(4, 576, 128)
    parts = lax.all_to_all(both, "x", 0, 0, tiled=True)
    turned = call(sum_kernel, "sum_x", S((16, 4, 8, 144), BF), n_in=1)(parts)
    pieces = lax.all_to_all(turned.reshape(64, 8, 144), ("y", "zh", "zl"), 0, 0, tiled=True)

    place = jnp.stack([core, x, zl, space]).astype(jnp.int32)
    output, grad_input, pen, rows = call(
        conv_kernel,
        "conv",
        (S((R, Q, CH), BF), S((ROWS, COLS, CH), BF), S((8, 144), F32), S((16, 1), F32)),
        scratch=[pltpu.VMEM((CH, 9 * CH), BF), pltpu.VMEM((4, POS, CH), F32), pltpu.VMEM((POS, CH), F32)],
        n_scalar=1,
        n_in=10,
    )(place, mine, other, up, low, cotangent, cot_s, ee, eo, oe, oo)
    own = jnp.sum(pieces.astype(F32), axis=0) / (R * n_space) + (4.0 * PEN_WEIGHT) * pen
    grad_kernel = jnp.transpose(own.reshape(8, 9, 16), (2, 1, 0)).reshape(16, 3, 3, 8)
    return output[None], grad_input[None], grad_kernel, rows.reshape(16)


def solution(mesh):
    fine = Mesh(mesh.devices.reshape(4, 4, 8, 2, 2), ("x", "zl", "y", "zh", "core"))
    fsdp, space = ("x", "zl"), ("y", "zh", "core")
    in_specs = (
        P(fsdp, space, None, None),
        P(fsdp, None, None, None),
        P(fsdp, space, None, None),
    )
    out_specs = (
        P(fsdp, space, None, None),
        P(fsdp, space, None, None),
        P(fsdp, None, None, space),
        P(fsdp),
    )
    return jax.shard_map(
        per_device, mesh=fine, in_specs=in_specs, out_specs=out_specs, check_vma=False
    )
```

```python
import jax
import jax.numpy as jnp
from jax import lax
from jax.experimental import pallas as pl
from jax.experimental.pallas import tpu as pltpu
from jax.sharding import Mesh, PartitionSpec as P

PEN_WEIGHT = 4.0
BF = jnp.bfloat16
F32 = jnp.float32

ROWS, COLS, CH = 24, 128, 256
R, Q = 12, 64
POS = R * Q
TAPS = [(i, j) for i in range(3) for j in range(3)]
SHIFTS = [(u, v) for u in (-2, 0, 2) for v in (-2, 0, 2)]

NT = (((1,), (1,)), ((), ()))


def mm(a, b):
    return jnp.dot(a, b, preferred_element_type=F32)


def mm_nt(a, b):
    return lax.dot_general(a, b, NT, preferred_element_type=F32)


def one_hot(cond):
    return jnp.where(cond, 1.0, 0.0).astype(BF)


def iota2(shape, axis):
    return lax.broadcasted_iota(jnp.int32, shape, axis)


def column_sorter():
    row, col = iota2((COLS, COLS), 0), iota2((COLS, COLS), 1)
    return one_hot(col == 2 * (row % Q) + row // Q)


def shift_left(block):
    moved = pltpu.roll(block, Q - 1, 0)
    return jnp.where(iota2(block.shape, 0) == Q - 1, 0.0, moved)


def shift_right(block):
    moved = pltpu.roll(block, 1, 0)
    return jnp.where(iota2(block.shape, 0) == 0, 0.0, moved)


def prep_kernel(
    core_ref, img_ref, cot_ref,
    per_ref, turn_ref, turn_low_ref,
    cot_s_ref,
):
    core = core_ref[0]
    sorter = column_sorter()
    chan, slot = iota2((CH, CH), 0), iota2((CH, CH), 1)
    other = jnp.where((chan // 8) % 2 == core, 0, 1)
    to_core = one_hot(slot == (chan // 16) * 8 + chan % 8 + (CH // 2) * other)
    for r in range(R):
        for parity in range(2):
            split = mm(sorter, img_ref[2 * r + parity]).astype(BF)
            per_ref[2 * parity, r * Q : (r + 1) * Q] = split[:Q]
            per_ref[2 * parity + 1, r * Q : (r + 1) * Q] = split[Q:]
    for k in range(4):
        per_ref[k] = mm(per_ref[k], to_core).astype(BF)
    for r in range(R):
        cot_s_ref[r * Q : (r + 1) * Q] = shift_left(cot_ref[r].astype(F32)).astype(BF)
    turn_ref[0] = cot_ref[...].reshape(POS, CH).T
    turn_ref[1] = cot_s_ref[...].T
    turn_low_ref[0] = cot_ref[1:].reshape(POS - Q, CH).T
    turn_low_ref[1] = cot_s_ref[Q:].T


def wgrad_kernel(low_ref, per_ref, turn_ref, turn_low_ref, keep_ref, send_ref):
    low = low_ref[...].astype(F32)
    low_t = (low.T.astype(BF), shift_left(low).T.astype(BF))
    for t, (i, j) in enumerate(TAPS):
        moved = 1 if j == 0 else 0
        image = (0 if i == 1 else 2) + (0 if j == 1 else 1)
        if i == 0:
            tap = mm(turn_low_ref[moved], per_ref[image, : POS - Q]) + mm(low_t[moved], per_ref[image, POS - Q :])
        else:
            tap = mm(turn_ref[moved], per_ref[image])
        tap = tap.reshape(16, 16, CH)
        keep_ref[:, t] = tap[:, :, : CH // 2]
        send_ref[:, t] = tap[:, :, CH // 2 :].astype(BF)


def back_kernel(
    place_ref, mine_ref, other_ref, low_ref, cot_ref,
    gin_ref, w_ref, pen_ref, row_ref,
    acc_ref, cot_s_ref,
):
    core, x, zl, space = place_ref[0], place_ref[1], place_ref[2], place_ref[3]
    half = CH // 2

    def halves(lower_ref, upper_ref):
        for t in range(9):
            lanes = slice(t * half, (t + 1) * half)
            w_ref[:, t * CH : t * CH + half] = lower_ref[:, lanes]
            w_ref[:, t * CH + half : (t + 1) * CH] = upper_ref[:, lanes]

    @pl.when(core == 0)
    def _():
        halves(mine_ref, other_ref)

    @pl.when(core == 1)
    def _():
        halves(other_ref, mine_ref)

    def tap(i, j):
        t = 3 * i + j
        return w_ref[:, t * CH : (t + 1) * CH]

    cot = cot_ref[...].reshape(POS, CH)
    below = jnp.concatenate([cot[Q:], low_ref[...]], axis=0)
    for r in range(R):
        cot_s_ref[r * Q : (r + 1) * Q] = shift_left(cot_ref[r].astype(F32)).astype(BF)
    cot_s = cot_s_ref[...]
    below_s = jnp.concatenate([cot_s[Q:], shift_left(low_ref[...].astype(F32)).astype(BF)], axis=0)
    acc_ref[0] = mm(cot, tap(1, 1))
    acc_ref[1] = mm(cot, tap(1, 2))
    acc_ref[1] += mm(cot_s, tap(1, 0))
    acc_ref[2] = mm(cot, tap(2, 1))
    acc_ref[2] += mm(below, tap(0, 1))
    acc_ref[3] = mm(cot, tap(2, 2))
    acc_ref[3] += mm(cot_s, tap(2, 0))
    acc_ref[3] += mm(below, tap(0, 2))
    acc_ref[3] += mm(below_s, tap(0, 0))
    row, col = iota2((COLS, COLS), 0), iota2((COLS, COLS), 1)
    weaver = one_hot(col == (row % 2) * Q + row // 2)
    for r in range(R):
        rows = slice(r * Q, (r + 1) * Q)
        for parity in range(2):
            both = jnp.concatenate(
                [acc_ref[2 * parity, rows].astype(BF), acc_ref[2 * parity + 1, rows].astype(BF)], axis=0
            )
            gin_ref[2 * r + parity] = mm(weaver, both).astype(BF)
    own_first = pl.multiple_of((x * 4 + zl) * 16, 16)
    own = [w_ref[pl.ds(own_first, 16), t * CH : (t + 1) * CH] for t in range(9)]
    grams = {}
    kin = [[s for s in range(9) if (s // 3 - t // 3) % 2 == 0 and (s % 3 - t % 3) % 2 == 0] for t in range(9)]
    for t in range(9):
        stacked = jnp.concatenate([own[s] for s in kin[t]], axis=0)
        part = mm_nt(stacked, w_ref[:, t * CH : (t + 1) * CH])
        for n, s in enumerate(kin[t]):
            shift = (s // 3 - t // 3, s % 3 - t % 3)
            block = part[n * 16 : (n + 1) * 16]
            grams[shift] = grams[shift] + block if shift in grams else block
    diagonal = iota2((16, CH), 0) + own_first == iota2((16, CH), 1)
    grams[(0, 0)] = grams[(0, 0)] - jnp.where(diagonal, 1.0, 0.0)
    squares = jnp.zeros((16, CH), F32)
    for shift in SHIFTS:
        squares = squares + grams[shift] * grams[shift]
    row_ref[...] = jnp.sum(squares.T, axis=0, keepdims=True)
    pieces = {}
    for shift in SHIFTS:
        high = grams[shift].astype(BF)
        rest = grams[shift] - high.astype(F32)
        pieces[shift] = (high, rest.astype(BF))
    grads = [jnp.zeros((16, CH), F32) for _ in range(9)]
    for s in range(9):
        stacked = jnp.concatenate(
            [pieces[(t // 3 - s // 3, t % 3 - s % 3)][p] for t in kin[s] for p in range(2)], axis=0
        )
        part = mm(stacked, w_ref[:, s * CH : (s + 1) * CH])
        for n, t in enumerate(kin[s]):
            for p in range(2):
                grads[t] = grads[t] + part[(2 * n + p) * 16 : (2 * n + p + 1) * 16]
    stacked = jnp.concatenate(grads, axis=0)
    high = stacked.astype(BF)
    rest = stacked - high.astype(F32)
    mid = rest.astype(BF)
    low = (rest - mid.astype(F32)).astype(BF)
    pick = one_hot(iota2((8, CH), 0) + space * 8 == iota2((8, CH), 1))
    pen_ref[...] = mm_nt(pick, high) + mm_nt(pick, mid) + mm_nt(pick, low)


def fore_kernel(w_ref, up_ref, img_ref, out_ref, ee_ref, eo_ref, oe_ref, oo_ref, acc_ref, z_ref):
    def tap(i, j):
        t = 3 * i + j
        return w_ref[:, t * CH : (t + 1) * CH]

    sorter = column_sorter()
    for r in range(R):
        rows = slice(r * Q, (r + 1) * Q)
        for parity, (even_ref, odd_ref) in enumerate(((ee_ref, eo_ref), (oe_ref, oo_ref))):
            split = mm(sorter, img_ref[2 * r + parity]).astype(BF)
            even_ref[rows] = split[:Q]
            odd_ref[rows] = split[Q:]
    halo = mm(sorter, up_ref[...]).astype(BF)
    oe_up = jnp.concatenate([halo[:Q], oe_ref[0 : POS - Q]], axis=0)
    oo_up = jnp.concatenate([halo[Q:], oo_ref[0 : POS - Q]], axis=0)
    z_ref[...] = mm_nt(eo_ref[...], tap(1, 0))
    z_ref[...] += mm_nt(oo_ref[...], tap(2, 0))
    z_ref[...] += mm_nt(oo_up, tap(0, 0))
    acc_ref[...] = mm_nt(ee_ref[...], tap(1, 1))
    acc_ref[...] += mm_nt(eo_ref[...], tap(1, 2))
    acc_ref[...] += mm_nt(oe_ref[...], tap(2, 1))
    acc_ref[...] += mm_nt(oo_ref[...], tap(2, 2))
    acc_ref[...] += mm_nt(oe_up, tap(0, 1))
    acc_ref[...] += mm_nt(oo_up, tap(0, 2))
    for r in range(R):
        rows = slice(r * Q, (r + 1) * Q)
        out_ref[r] = (acc_ref[rows] + shift_right(z_ref[rows])).astype(BF)


def sum_kernel(parts_ref, out_ref):
    total = parts_ref[0].astype(F32)
    for k in range(1, 4):
        total = total + parts_ref[k].astype(F32)
    turned = total.T
    for k in range(4):
        out_ref[:, k] = turned[:, 144 * k : 144 * (k + 1)].reshape(16, 8, 144).astype(BF)


def call(kernel, out_shape, scratch=(), n_scalar=0, n_in=0):
    vmem = pl.BlockSpec(memory_space=pltpu.VMEM)
    smem = pl.BlockSpec(memory_space=pltpu.SMEM)
    many = isinstance(out_shape, (tuple, list))
    return pl.pallas_call(
        kernel,
        out_shape=out_shape,
        in_specs=[smem] * n_scalar + [vmem] * n_in,
        out_specs=tuple(vmem for _ in out_shape) if many else vmem,
        scratch_shapes=list(scratch),
        compiler_params=pltpu.CompilerParams(vmem_limit_bytes=24 * 1024 * 1024),
    )


def spread(block, axis, size):
    return lax.all_to_all(jnp.broadcast_to(block[None], (size,) + block.shape), axis, 0, 0, tiled=True)


def per_device(images, kernel, cotangent):
    return body(images[0], kernel, cotangent[0])


def body(images, kernel, cotangent):
    S = jax.ShapeDtypeStruct
    core, x, zl = lax.axis_index("core"), lax.axis_index("x"), lax.axis_index("zl")
    space = lax.axis_index(("y", "zh", "core"))
    n_space = 32
    swap = [(0, 1), (1, 0)]
    panel = lax.dynamic_index_in_dim(kernel.reshape(16, 9, 2, CH // 2), core, 2, keepdims=False)
    own = spread(panel.reshape(16, 9 * CH // 2), "zl", 4).reshape(64, 9 * CH // 2)
    mine = spread(own, "x", 4).reshape(256, 9 * CH // 2)
    low = lax.ppermute(cotangent[0], ("y", "zh", "core"), [(i + 1, i) for i in range(n_space - 1)])
    per, turn, turn_low = call(
        prep_kernel,
        (S((4, POS, CH), BF), S((2, CH, POS), BF), S((2, CH, POS - Q), BF)),
        scratch=[pltpu.VMEM((POS, CH), BF)],
        n_scalar=1,
        n_in=2,
    )(core.astype(jnp.int32).reshape(1), images, cotangent)
    keep, send = call(
        wgrad_kernel, (S((16, 9, 16, 128), F32), S((16, 9, 16, 128), BF)), n_in=4
    )(low, per, turn, turn_low)
    recv = lax.ppermute(send, "core", swap)
    both = (keep + recv.astype(F32)).astype(BF).reshape(4, 576, 128)
    parts = lax.all_to_all(both, "x", 0, 0, tiled=True)
    turned = call(sum_kernel, S((16, 4, 8, 144), BF), n_in=1)(parts)
    pieces = lax.all_to_all(turned.reshape(64, 8, 144), ("y", "zh", "zl"), 0, 0, tiled=True)
    up = lax.ppermute(images[ROWS - 1], ("y", "zh", "core"), [(i, i + 1) for i in range(n_space - 1)])
    other = lax.ppermute(mine, "core", swap)
    place = jnp.stack([core, x, zl, space]).astype(jnp.int32)
    grad_input, whole, pen, rows = call(
        back_kernel,
        (S((ROWS, COLS, CH), BF), S((CH, 9 * CH), BF), S((8, 144), F32), S((1, 16), F32)),
        scratch=[pltpu.VMEM((4, POS, CH), F32), pltpu.VMEM((POS, CH), BF)],
        n_scalar=1,
        n_in=4,
    )(place, mine, other, low, cotangent)
    output = call(
        fore_kernel,
        S((R, Q, CH), BF),
        scratch=[pltpu.VMEM((POS, CH), BF)] * 4 + [pltpu.VMEM((POS, CH), F32)] * 2,
        n_in=3,
    )(whole, up, images)
    own = jnp.sum(pieces.astype(F32), axis=0) / (R * n_space) + (4.0 * PEN_WEIGHT) * pen
    grad_kernel = jnp.transpose(own.reshape(8, 9, 16), (2, 1, 0)).reshape(16, 3, 3, 8)
    return output[None], grad_input[None], grad_kernel, rows.reshape(16)


def solution(mesh):
    fine = Mesh(mesh.devices.reshape(4, 4, 8, 2, 2), ("x", "zl", "y", "zh", "core"))
    fsdp, space = ("x", "zl"), ("y", "zh", "core")
    in_specs = (
        P(fsdp, space, None, None),
        P(fsdp, None, None, None),
        P(fsdp, space, None, None),
    )
    out_specs = (
        P(fsdp, space, None, None),
        P(fsdp, space, None, None),
        P(fsdp, None, None, space),
        P(fsdp),
    )
    return jax.shard_map(
        per_device, mesh=fine, in_specs=in_specs, out_specs=out_specs, check_vma=False
    )
```

```python
import jax
import jax.numpy as jnp
from jax import lax
from jax.experimental import pallas as pl
from jax.experimental.pallas import tpu as pltpu
from jax.sharding import Mesh, PartitionSpec as P

PEN_WEIGHT = 4.0
BF = jnp.bfloat16
F32 = jnp.float32

ROWS, COLS, CH = 24, 128, 256
R, Q = 12, 64
POS = R * Q
TAPS = [(i, j) for i in range(3) for j in range(3)]
SHIFTS = [(u, v) for u in (-2, 0, 2) for v in (-2, 0, 2)]

NT = (((1,), (1,)), ((), ()))


def mm(a, b):
    return jnp.dot(a, b, preferred_element_type=F32)


def mm_nt(a, b):
    return lax.dot_general(a, b, NT, preferred_element_type=F32)


def one_hot(cond):
    return jnp.where(cond, 1.0, 0.0).astype(BF)


def iota2(shape, axis):
    return lax.broadcasted_iota(jnp.int32, shape, axis)


def column_sorter():
    row, col = iota2((COLS, COLS), 0), iota2((COLS, COLS), 1)
    return one_hot(col == 2 * (row % Q) + row // Q)


def shift_left(block):
    moved = pltpu.roll(block, Q - 1, 0)
    return jnp.where(iota2(block.shape, 0) == Q - 1, 0.0, moved)


def shift_right(block):
    moved = pltpu.roll(block, 1, 0)
    return jnp.where(iota2(block.shape, 0) == 0, 0.0, moved)


def prep_kernel(
    core_ref, img_ref, cot_ref,
    per_ref, turn_ref, turn_low_ref,
    cot_s_ref,
):
    core = core_ref[0]
    sorter = column_sorter()
    chan, slot = iota2((CH, CH), 0), iota2((CH, CH), 1)
    other = jnp.where((chan // 8) % 2 == core, 0, 1)
    to_core = one_hot(slot == (chan // 16) * 8 + chan % 8 + (CH // 2) * other)
    for r in range(R):
        for parity in range(2):
            split = mm(sorter, img_ref[2 * r + parity]).astype(BF)
            per_ref[2 * parity, r * Q : (r + 1) * Q] = split[:Q]
            per_ref[2 * parity + 1, r * Q : (r + 1) * Q] = split[Q:]
    for k in range(4):
        per_ref[k] = mm(per_ref[k], to_core).astype(BF)
    for r in range(R):
        cot_s_ref[r * Q : (r + 1) * Q] = shift_left(cot_ref[r].astype(F32)).astype(BF)
    turn_ref[0] = cot_ref[...].reshape(POS, CH).T
    turn_ref[1] = cot_s_ref[...].T
    turn_low_ref[0] = cot_ref[1:].reshape(POS - Q, CH).T
    turn_low_ref[1] = cot_s_ref[Q:].T


def wgrad_kernel(low_ref, per_ref, turn_ref, turn_low_ref, keep_ref, send_ref):
    low = low_ref[...].astype(F32)
    low_t = (low.T.astype(BF), shift_left(low).T.astype(BF))
    for t, (i, j) in enumerate(TAPS):
        moved = 1 if j == 0 else 0
        image = (0 if i == 1 else 2) + (0 if j == 1 else 1)
        if i == 0:
            tap = mm(turn_low_ref[moved], per_ref[image, : POS - Q]) + mm(low_t[moved], per_ref[image, POS - Q :])
        else:
            tap = mm(turn_ref[moved], per_ref[image])
        tap = tap.reshape(16, 16, CH)
        keep_ref[:, t] = tap[:, :, : CH // 2]
        send_ref[:, t] = tap[:, :, CH // 2 :].astype(BF)


def back_kernel(
    place_ref, mine_ref, other_ref, low_ref, cot_ref,
    gin_ref, w_ref, pen_ref, row_ref,
    acc_ref, cot_s_ref,
):
    core, x, zl, space = place_ref[0], place_ref[1], place_ref[2], place_ref[3]
    half = CH // 2

    def halves(lower_ref, upper_ref):
        for f in range(16):
            rows = slice(f * 16, (f + 1) * 16)
            for t in range(9):
                w_ref[rows, t * CH : t * CH + half] = lower_ref[f, t]
                w_ref[rows, t * CH + half : (t + 1) * CH] = upper_ref[f, t]

    @pl.when(core == 0)
    def _():
        halves(mine_ref, other_ref)

    @pl.when(core == 1)
    def _():
        halves(other_ref, mine_ref)

    def tap(i, j):
        t = 3 * i + j
        return w_ref[:, t * CH : (t + 1) * CH]

    cot = cot_ref[...].reshape(POS, CH)
    below = jnp.concatenate([cot[Q:], low_ref[...]], axis=0)
    for r in range(R):
        cot_s_ref[r * Q : (r + 1) * Q] = shift_left(cot_ref[r].astype(F32)).astype(BF)
    cot_s = cot_s_ref[...]
    below_s = jnp.concatenate([cot_s[Q:], shift_left(low_ref[...].astype(F32)).astype(BF)], axis=0)
    acc_ref[0] = mm(cot, tap(1, 1))
    acc_ref[1] = mm(cot, tap(1, 2))
    acc_ref[1] += mm(cot_s, tap(1, 0))
    acc_ref[2] = mm(cot, tap(2, 1))
    acc_ref[2] += mm(below, tap(0, 1))
    acc_ref[3] = mm(cot, tap(2, 2))
    acc_ref[3] += mm(cot_s, tap(2, 0))
    acc_ref[3] += mm(below, tap(0, 2))
    acc_ref[3] += mm(below_s, tap(0, 0))
    row, col = iota2((COLS, COLS), 0), iota2((COLS, COLS), 1)
    weaver = one_hot(col == (row % 2) * Q + row // 2)
    for r in range(R):
        rows = slice(r * Q, (r + 1) * Q)
        for parity in range(2):
            both = jnp.concatenate(
                [acc_ref[2 * parity, rows].astype(BF), acc_ref[2 * parity + 1, rows].astype(BF)], axis=0
            )
            gin_ref[2 * r + parity] = mm(weaver, both).astype(BF)
    own_first = pl.multiple_of((x * 4 + zl) * 16, 16)
    own = [w_ref[pl.ds(own_first, 16), t * CH : (t + 1) * CH] for t in range(9)]
    grams = {}
    kin = [[s for s in range(9) if (s // 3 - t // 3) % 2 == 0 and (s % 3 - t % 3) % 2 == 0] for t in range(9)]
    for t in range(9):
        stacked = jnp.concatenate([own[s] for s in kin[t]], axis=0)
        part = mm_nt(stacked, w_ref[:, t * CH : (t + 1) * CH])
        for n, s in enumerate(kin[t]):
            shift = (s // 3 - t // 3, s % 3 - t % 3)
            block = part[n * 16 : (n + 1) * 16]
            grams[shift] = grams[shift] + block if shift in grams else block
    diagonal = iota2((16, CH), 0) + own_first == iota2((16, CH), 1)
    grams[(0, 0)] = grams[(0, 0)] - jnp.where(diagonal, 1.0, 0.0)
    squares = jnp.zeros((16, CH), F32)
    for shift in SHIFTS:
        squares = squares + grams[shift] * grams[shift]
    row_ref[...] = jnp.sum(squares.T, axis=0, keepdims=True)
    pieces = {}
    for shift in SHIFTS:
        high = grams[shift].astype(BF)
        rest = grams[shift] - high.astype(F32)
        pieces[shift] = (high, rest.astype(BF))
    grads = [jnp.zeros((16, CH), F32) for _ in range(9)]
    for s in range(9):
        stacked = jnp.concatenate(
            [pieces[(t // 3 - s // 3, t % 3 - s % 3)][p] for t in kin[s] for p in range(2)], axis=0
        )
        part = mm(stacked, w_ref[:, s * CH : (s + 1) * CH])
        for n, t in enumerate(kin[s]):
            for p in range(2):
                grads[t] = grads[t] + part[(2 * n + p) * 16 : (2 * n + p + 1) * 16]
    stacked = jnp.concatenate(grads, axis=0)
    high = stacked.astype(BF)
    rest = stacked - high.astype(F32)
    mid = rest.astype(BF)
    low = (rest - mid.astype(F32)).astype(BF)
    pick = one_hot(iota2((8, CH), 0) + space * 8 == iota2((8, CH), 1))
    pen_ref[...] = mm_nt(pick, high) + mm_nt(pick, mid) + mm_nt(pick, low)


def fore_kernel(w_ref, up_ref, img_ref, out_ref, ee_ref, eo_ref, oe_ref, oo_ref, acc_ref, z_ref):
    def tap(i, j):
        t = 3 * i + j
        return w_ref[:, t * CH : (t + 1) * CH]

    sorter = column_sorter()
    for r in range(R):
        rows = slice(r * Q, (r + 1) * Q)
        for parity, (even_ref, odd_ref) in enumerate(((ee_ref, eo_ref), (oe_ref, oo_ref))):
            split = mm(sorter, img_ref[2 * r + parity]).astype(BF)
            even_ref[rows] = split[:Q]
            odd_ref[rows] = split[Q:]
    halo = mm(sorter, up_ref[...]).astype(BF)
    oe_up = jnp.concatenate([halo[:Q], oe_ref[0 : POS - Q]], axis=0)
    oo_up = jnp.concatenate([halo[Q:], oo_ref[0 : POS - Q]], axis=0)
    z_ref[...] = mm_nt(eo_ref[...], tap(1, 0))
    z_ref[...] += mm_nt(oo_ref[...], tap(2, 0))
    z_ref[...] += mm_nt(oo_up, tap(0, 0))
    acc_ref[...] = mm_nt(ee_ref[...], tap(1, 1))
    acc_ref[...] += mm_nt(eo_ref[...], tap(1, 2))
    acc_ref[...] += mm_nt(oe_ref[...], tap(2, 1))
    acc_ref[...] += mm_nt(oo_ref[...], tap(2, 2))
    acc_ref[...] += mm_nt(oe_up, tap(0, 1))
    acc_ref[...] += mm_nt(oo_up, tap(0, 2))
    for r in range(R):
        rows = slice(r * Q, (r + 1) * Q)
        out_ref[r] = (acc_ref[rows] + shift_right(z_ref[rows])).astype(BF)


def sum_kernel(parts_ref, out_ref):
    total = parts_ref[0].astype(F32)
    for k in range(1, 4):
        total = total + parts_ref[k].astype(F32)
    turned = total.T
    for k in range(4):
        block = turned[:, 144 * k : 144 * (k + 1)].reshape(16, 8, 144)
        out_ref[:, k, :, :144] = block[:, :4].astype(BF)
        out_ref[:, k, :, 144:] = block[:, 4:].astype(BF)


def panel_kernel(core_ref, kernel_ref, out_ref):
    @pl.when(core_ref[0] == 0)
    def _():
        for k in range(4):
            out_ref[k] = kernel_ref[:, :, : CH // 2]

    @pl.when(core_ref[0] == 1)
    def _():
        for k in range(4):
            out_ref[k] = kernel_ref[:, :, CH // 2 :]


def final_kernel(parts_ref, pen_ref, out_ref):
    both = jnp.sum(parts_ref[...].astype(F32), axis=0)
    total = jnp.concatenate([both[:, :144], both[:, 144:]], axis=0) / (R * 32) + (4.0 * PEN_WEIGHT) * pen_ref[...]
    for t in range(9):
        out_ref[t] = total[:, 16 * t : 16 * (t + 1)]


def call(kernel, out_shape, scratch=(), n_scalar=0, n_in=0):
    vmem = pl.BlockSpec(memory_space=pltpu.VMEM)
    smem = pl.BlockSpec(memory_space=pltpu.SMEM)
    many = isinstance(out_shape, (tuple, list))
    return pl.pallas_call(
        kernel,
        out_shape=out_shape,
        in_specs=[smem] * n_scalar + [vmem] * n_in,
        out_specs=tuple(vmem for _ in out_shape) if many else vmem,
        scratch_shapes=list(scratch),
        compiler_params=pltpu.CompilerParams(vmem_limit_bytes=24 * 1024 * 1024),
    )


def spread(block, axis, size):
    return lax.all_to_all(jnp.broadcast_to(block[None], (size,) + block.shape), axis, 0, 0, tiled=True)


def per_device(images, kernel, cotangent):
    return body(images[0], kernel, cotangent[0])


def body(images, kernel, cotangent):
    S = jax.ShapeDtypeStruct
    core, x, zl = lax.axis_index("core"), lax.axis_index("x"), lax.axis_index("zl")
    space = lax.axis_index(("y", "zh", "core"))
    n_space = 32
    swap = [(0, 1), (1, 0)]
    panel = jnp.transpose(kernel, (1, 2, 0, 3)).reshape(9, 16, CH)
    panels = call(panel_kernel, S((4, 9, 16, CH // 2), BF), n_scalar=1, n_in=1)(
        core.astype(jnp.int32).reshape(1), panel
    )
    own = lax.all_to_all(panels, "zl", 0, 0, tiled=True)
    mine = spread(own, "x", 4).reshape(16, 9, 16, CH // 2)
    low = lax.ppermute(cotangent[0], ("y", "zh", "core"), [(i + 1, i) for i in range(n_space - 1)])
    per, turn, turn_low = call(
        prep_kernel,
        (S((4, POS, CH), BF), S((2, CH, POS), BF), S((2, CH, POS - Q), BF)),
        scratch=[pltpu.VMEM((POS, CH), BF)],
        n_scalar=1,
        n_in=2,
    )(core.astype(jnp.int32).reshape(1), images, cotangent)
    keep, send = call(
        wgrad_kernel, (S((16, 9, 16, 128), F32), S((16, 9, 16, 128), BF)), n_in=4
    )(low, per, turn, turn_low)
    recv = lax.ppermute(send, "core", swap)
    both = (keep + recv.astype(F32)).astype(BF).reshape(4, 576, 128)
    parts = lax.all_to_all(both, "x", 0, 0, tiled=True)
    turned = call(sum_kernel, S((16, 4, 4, 288), BF), n_in=1)(parts)
    pieces = lax.all_to_all(turned.reshape(64, 4, 288), ("y", "zh", "zl"), 0, 0, tiled=True)
    up = lax.ppermute(images[ROWS - 1], ("y", "zh", "core"), [(i, i + 1) for i in range(n_space - 1)])
    other = lax.ppermute(mine, "core", swap)
    place = jnp.stack([core, x, zl, space]).astype(jnp.int32)
    grad_input, whole, pen, rows = call(
        back_kernel,
        (S((ROWS, COLS, CH), BF), S((CH, 9 * CH), BF), S((8, 144), F32), S((1, 16), F32)),
        scratch=[pltpu.VMEM((4, POS, CH), F32), pltpu.VMEM((POS, CH), BF)],
        n_scalar=1,
        n_in=4,
    )(place, mine, other, low, cotangent)
    output = call(
        fore_kernel,
        S((R, Q, CH), BF),
        scratch=[pltpu.VMEM((POS, CH), BF)] * 4 + [pltpu.VMEM((POS, CH), F32)] * 2,
        n_in=3,
    )(whole, up, images)
    grads = call(final_kernel, S((9, 8, 16), F32), n_in=2)(pieces, pen)
    grad_kernel = jnp.transpose(grads.reshape(3, 3, 8, 16), (3, 0, 1, 2))
    return output[None], grad_input[None], grad_kernel, rows.reshape(16)


def solution(mesh):
    fine = Mesh(mesh.devices.reshape(4, 4, 8, 2, 2), ("x", "zl", "y", "zh", "core"))
    fsdp, space = ("x", "zl"), ("y", "zh", "core")
    in_specs = (
        P(fsdp, space, None, None),
        P(fsdp, None, None, None),
        P(fsdp, space, None, None),
    )
    out_specs = (
        P(fsdp, space, None, None),
        P(fsdp, space, None, None),
        P(fsdp, None, None, space),
        P(fsdp),
    )
    return jax.shard_map(
        per_device, mesh=fine, in_specs=in_specs, out_specs=out_specs, check_vma=False
    )
```
